32 devices in a mesh: bx: 8 (over y, x, core), by: 4 (over z).
Axes of the slice: x: 2, y: 2, z: 4, core: 2. Of those that a mesh axis runs over, the one named last changes fastest.
Arguments:
- interface_velocity: float32 [3, 2048, 2048], P(None, 'bx', 'by'), may hold values from -6 to 6
- history: float32 [6, 2, 3, 256, 8, 4, 512], P(None, None, None, 'by', 'bx'), may hold values from -6 to 6
- kernel: float32 [7, 256, 8, 4, 512], P(None, 'by', 'bx'), may hold values from -6 to 6
- velocity: float32 [3, 4, 2048, 2048], P(None, None, 'bx', 'by'), may hold values from -6 to 6
- stress: float32 [6, 4, 2048, 2048], P(None, None, 'bx', 'by'), may hold values from -6 to 6
- cohesion: float32 [4, 2048, 2048], P(None, 'bx', 'by'), may hold values from 0.5 to 4
Outputs:
- velocity_new: float32 [3, 4, 2048, 2048], P(None, None, 'bx', 'by')
- stress_new: float32 [6, 4, 2048, 2048], P(None, None, 'bx', 'by')
The draws below stay inside these ranges and needn't reach their ends.
All inputs are finite; a program needn't handle non-finite values.
Results may differ from the reference program's by a relative error of at most 0.00005.
Values sent between devices are 32-bit elements; how exact they have to be, the bound alone decides.
A program may use at most 192 MiB of HBM per device.

```python
import math
import jax
import jax.numpy as jnp
from jax import lax

NX = 2048
NY = 2048
NZ = 4
HIST = 6
CX = 256
CY = 512
STRIKE_PARTS = 8
DIP_PARTS = 4


def block_scale(key, dims, cuts, low, largest):
    level, own = 1.0, jax.random.fold_in(key, 6)
    for dim, shards_of in cuts:
        steps = jnp.exp(jax.random.uniform(jax.random.fold_in(own, dim), (shards_of,), jnp.float32, low / len(cuts), largest / len(cuts)))
        level = level * jnp.repeat(steps, dims[dim] // shards_of).reshape([-1 if axis == dim else 1 for axis in range(len(dims))])
    return level


def centred(key, shape, scale, bound, cuts=(), dtype=jnp.bfloat16):
    result = jax.random.normal(key, shape, jnp.float32) * scale
    if len(cuts) > 0:
        result = block_scale(key, shape, cuts, -0.22, 0.18) * result
    return jnp.clip(result, min=-bound, max=bound).astype(dtype)


def setup_inputs(seed: int = 0) -> dict:
    splits = jax.random.split(jax.random.key(seed), 7)
    return {
        "interface_velocity": centred(splits[0], (3, NX, NY), 1.0, 6.0, ((1, 8), (2, 4)), jnp.float32),
        "history": centred(splits[1], (HIST, 2, 3, CX, STRIKE_PARTS, DIP_PARTS, CY), 1.0, 6.0, ((3, 4), (4, 8)), jnp.float32),
        "kernel": centred(splits[2], (HIST + 1, CX, STRIKE_PARTS, DIP_PARTS, CY), ((HIST + 1) ** -0.5), 6.0, ((1, 4), (2, 8)), jnp.float32),
        "velocity": centred(splits[3], (3, NZ, NX, NY), 1.0, 6.0, ((2, 8), (3, 4)), jnp.float32),
        "stress": centred(splits[4], (6, NZ, NX, NY), 1.0, 6.0, ((2, 8), (3, 4)), jnp.float32),
        "cohesion": jnp.clip(jnp.exp(math.log(4.0) - 2.0794415 * jax.random.uniform(splits[5], (NZ, NX, NY), jnp.float32) ** block_scale(splits[5], (NZ, NX, NY), ((1, 8), (2, 4)), -0.2, 0.2)), 0.5, 4.0),
    }


COURANT = 0.3
FRICTION = 0.6

def to_layout(transform):
    stacked = jnp.stack([jnp.real(transform), jnp.imag(transform)])
    stacked = stacked.reshape(2, 3, CX, STRIKE_PARTS, CY, DIP_PARTS)
    return jnp.transpose(stacked, (0, 1, 2, 3, 5, 4))

def from_layout(stacked):
    ordered = jnp.transpose(stacked, (0, 1, 2, 3, 5, 4)).reshape(2, 3, NX, NY)
    return ordered[0] + 1j * ordered[1]

def strike_diff(padded):
    return 0.5 * (padded[..., 2:, 1:-1] - padded[..., :-2, 1:-1])

def dip_diff(padded):
    return 0.5 * (padded[..., 1:-1, 2:] - padded[..., 1:-1, :-2])

def depth_diff(layered, ghost_layer):
    above_layer = jnp.concatenate([layered[1:], jnp.zeros_like(layered[:1])], axis=0)
    below_layer = jnp.concatenate([ghost_layer[None], layered[:-1]], axis=0)
    return 0.5 * (above_layer - below_layer)

def yield_limit(trial_stress, cohesion):
    pressure = (trial_stress[0] + trial_stress[1] + trial_stress[2]) / 3.0
    normal_dev = trial_stress[:3] - pressure[None]
    second = 0.5 * lax.optimization_barrier(jnp.sum(normal_dev * normal_dev, axis=0)) + lax.optimization_barrier(jnp.sum(trial_stress[3:] * trial_stress[3:], axis=0))
    shear_stress = jnp.sqrt(second)
    yield_stress = cohesion + FRICTION * jnp.maximum(-pressure, 0.0)
    factor = yield_stress / jnp.maximum(shear_stress, yield_stress)
    return jnp.concatenate([pressure[None] + factor[None] * normal_dev, factor[None] * trial_stress[3:]], axis=0)

def advance_bulk(velocity, stress, traction, interface_velocity, cohesion, widen):
    padded_stress = widen(stress)
    forcing = jnp.stack([strike_diff(padded_stress[0]) + dip_diff(padded_stress[3]) + depth_diff(stress[4], traction[0]), strike_diff(padded_stress[3]) + dip_diff(padded_stress[1]) + depth_diff(stress[5], traction[1]), strike_diff(padded_stress[4]) + dip_diff(padded_stress[5]) + depth_diff(stress[2], traction[2])])
    velocity_new = velocity + COURANT * forcing
    padded_velocity = widen(velocity_new)
    strike_grad = strike_diff(padded_velocity)
    dip_grad = dip_diff(padded_velocity)
    depth_grad = jnp.stack([depth_diff(velocity_new[component], interface_velocity[component]) for component in range(3)])
    dilation = strike_grad[0] + dip_grad[1] + depth_grad[2]
    rates = jnp.stack([dilation + 2.0 * strike_grad[0], dilation + 2.0 * dip_grad[1], dilation + 2.0 * depth_grad[2], dip_grad[0] + strike_grad[1], depth_grad[0] + strike_grad[2], depth_grad[1] + dip_grad[2]])
    trial_stress = stress + COURANT * rates
    return (velocity_new, yield_limit(trial_stress, cohesion))

def wrap_pad(fields):
    return jnp.pad(fields, ((0, 0), (0, 0), (1, 1), (1, 1)), mode='wrap')

def reference(interface_velocity, history, kernel, velocity, stress, cohesion):
    transform = jnp.fft.fft2(interface_velocity, axes=(1, 2), norm='ortho')
    spectrum = to_layout(transform).astype(jnp.float32)
    past_terms = jnp.einsum('hupks,hzcupks->zcupks', kernel[1:].astype(jnp.float32), history.astype(jnp.float32), precision=lax.Precision.HIGHEST)
    response = kernel[0][None, None] * spectrum + past_terms
    traction = jnp.real(jnp.fft.ifft2(from_layout(response), axes=(1, 2), norm='ortho')).astype(jnp.float32)
    velocity_new, stress_new = advance_bulk(velocity, stress, traction, interface_velocity, cohesion, wrap_pad)
    return (velocity_new, stress_new)
```

```python
from functools import partial
import math

import jax
import jax.numpy as jnp
import numpy as np
from jax import lax
from jax.experimental import pallas as pl
from jax.experimental.pallas import tpu as pltpu
from jax.sharding import PartitionSpec as P

COURANT = 0.3
FRICTION = 0.6
CHUNKS = 1
F32 = jnp.float32
BF16 = jnp.bfloat16


def halves(table):
    high = np.asarray(table, np.float32).astype(BF16)
    low = (np.asarray(table, np.float64) - high.astype(np.float64)).astype(BF16)
    return np.stack([high, low])


def square_table(length):
    index = np.arange(length)
    angle = 2.0 * math.pi / length * (index[:, None] * index[None, :] % length)
    return jnp.asarray(np.stack([halves(np.cos(angle)), halves(np.sin(angle))]))


def split(value):
    high = value.astype(BF16)
    return high, (value - high.astype(F32)).astype(BF16)


def product(value, table, left):
    def dot(a, b):
        if left:
            a, b = b, a
        return lax.dot_general(a, b, (((1,), (0,)), ((), ())), preferred_element_type=F32)

    return dot(value[0], table[0]) + (dot(value[0], table[1]) + dot(value[1], table[0]))


def complex_product(real_part, imag_part, table_ref, sign, left):
    cos = (table_ref[0, 0], table_ref[0, 1])
    sin = (table_ref[1, 0], table_ref[1, 1])
    real_part, imag_part = split(real_part), split(imag_part)
    return (
        product(real_part, cos, left) - sign * product(imag_part, sin, left),
        product(imag_part, cos, left) + sign * product(real_part, sin, left),
    )


def root(index, count):
    angle = 2.0 * math.pi * (index % count) / count
    cos, sin = math.cos(angle), math.sin(angle)
    return [float(round(v)) if abs(v - round(v)) < 1e-12 else v for v in (cos, sin)]


def add_term(total, factor, value):
    if factor == 0.0:
        return total
    term = value if factor == 1.0 else (-value if factor == -1.0 else factor * value)
    return term if total is None else total + term


def strike_forward(count, x_ref, o_ref):
    for c in range(x_ref.shape[1]):
        for r in range(count):
            real_part = imag_part = None
            for b in range(count):
                cos, sin = root(r * b, count)
                real_part = add_term(real_part, cos, x_ref[b, c])
                imag_part = add_term(imag_part, -sin, x_ref[b, c])
            o_ref[r, 0, c] = real_part
            o_ref[r, 1, c] = jnp.zeros_like(real_part) if imag_part is None else imag_part


def strike_inverse(count, scale, x_ref, o_ref):
    for c in range(x_ref.shape[2]):
        for b in range(count):
            total = None
            for r in range(count):
                cos, sin = root(r * b, count)
                total = add_term(total, cos, x_ref[r, 0, c])
                total = add_term(total, -sin, x_ref[r, 1, c])
            o_ref[b, c] = scale * total


def strike_cells_dft(sign, x_ref, tw_ref, table_ref, o_ref, held):
    blocks, _, _, rows, _ = x_ref.shape
    for s in range(blocks):
        for z in range(2):
            held[z, pl.ds(s * rows, rows), :] = x_ref[s, z, 0]
    cos, sin = tw_ref[:, 0:1], sign * tw_ref[:, 1:2]
    real_part, imag_part = held[0], held[1]
    if sign < 0:
        real_part, imag_part = (
            real_part * cos - imag_part * sin,
            real_part * sin + imag_part * cos,
        )
    real_part, imag_part = complex_product(real_part, imag_part, table_ref, sign, True)
    if sign > 0:
        real_part, imag_part = (
            real_part * cos - imag_part * sin,
            real_part * sin + imag_part * cos,
        )
    held[0] = real_part
    held[1] = imag_part
    blocks, _, _, rows, _ = o_ref.shape
    for s in range(blocks):
        for z in range(2):
            o_ref[s, z, 0] = held[z, pl.ds(s * rows, rows), :]


def dip_response(scale, x_ref, tw_ref, table_ref, now_ref, past_ref, o_ref, held):
    count, _, _, rows, _ = x_ref.shape
    for l in range(count):
        real_part = imag_part = None
        for j in range(count):
            cos, sin = root(l * j, count)
            real_part = add_term(real_part, cos, x_ref[j, 0, 0])
            real_part = add_term(real_part, sin, x_ref[j, 1, 0])
            imag_part = add_term(imag_part, cos, x_ref[j, 1, 0])
            imag_part = add_term(imag_part, -sin, x_ref[j, 0, 0])
        cos, sin = tw_ref[0, l : l + 1, :], tw_ref[1, l : l + 1, :]
        held[0, pl.ds(l * rows, rows), :] = real_part * cos + imag_part * sin
        held[1, pl.ds(l * rows, rows), :] = imag_part * cos - real_part * sin
    real_part, imag_part = complex_product(held[0], held[1], table_ref, -1.0, False)
    weight = scale * now_ref[...]
    real_part = weight * real_part + past_ref[0, 0]
    imag_part = weight * imag_part + past_ref[1, 0]
    real_part, imag_part = complex_product(real_part, imag_part, table_ref, 1.0, False)
    held[0] = real_part
    held[1] = imag_part
    for l in range(count):
        cos, sin = tw_ref[0, l : l + 1, :], tw_ref[1, l : l + 1, :]
        real_part = held[0, pl.ds(l * rows, rows), :]
        imag_part = held[1, pl.ds(l * rows, rows), :]
        held[0, pl.ds(l * rows, rows), :] = real_part * cos - imag_part * sin
        held[1, pl.ds(l * rows, rows), :] = imag_part * cos + real_part * sin
    for j in range(count):
        real_part = imag_part = None
        for l in range(count):
            cos, sin = root(l * j, count)
            lr = held[0, pl.ds(l * rows, rows), :]
            li = held[1, pl.ds(l * rows, rows), :]
            real_part = add_term(real_part, cos, lr)
            real_part = add_term(real_part, -sin, li)
            imag_part = add_term(imag_part, cos, li)
            imag_part = add_term(imag_part, sin, lr)
        o_ref[j, 0, 0] = real_part
        o_ref[j, 1, 0] = imag_part


def rows_diff(value, before, after):
    count = value.shape[0]
    row = lax.broadcasted_iota(jnp.int32, value.shape, 0)
    low = jnp.where(row == 0, before, pltpu.roll(value, 1, 0))
    high = jnp.where(row == count - 1, after, pltpu.roll(value, count - 1, 0))
    return 0.5 * (high - low)


def cols_diff(value, before, after):
    count = value.shape[1]
    col = lax.broadcasted_iota(jnp.int32, value.shape, 1)
    low = jnp.where(col == 0, before, pltpu.roll(value, 1, 1))
    high = jnp.where(col == count - 1, after, pltpu.roll(value, count - 1, 1))
    return 0.5 * (high - low)


def layer_diff(layers, ghost, z):
    low = ghost if z == 0 else layers(z - 1)
    return 0.5 * (layers(z + 1) - low)


def strike_edges(low_ref, prev_ref, high_ref, next_ref, slot, component, z):
    i, last = pl.program_id(0), pl.num_programs(0) - 1
    before = jnp.where(i == 0, low_ref[slot, z : z + 1, :], prev_ref[component, z, 7:8, :])
    after = jnp.where(i == last, high_ref[slot, z : z + 1, :], next_ref[component, z, 0:1, :])
    return before, after


def velocity_step(s_ref, prev_ref, next_ref, low_ref, high_ref, col_ref, v_ref, t_ref, o_ref, c_ref):
    layers = v_ref.shape[1]
    width = v_ref.shape[3]
    half = 3 * layers
    for component, (sx, sy, sz) in enumerate(((0, 3, 4), (3, 1, 5), (4, 5, 2))):
        for z in range(layers):
            before, after = strike_edges(low_ref, prev_ref, high_ref, next_ref, component, sx, z)
            total = rows_diff(s_ref[sx, z], before, after)
            k = component * layers + z
            total = total + cols_diff(
                s_ref[sy, z], col_ref[:, k : k + 1], col_ref[:, half + k : half + k + 1]
            )
            low = t_ref[component] if z == 0 else s_ref[sz, z - 1]
            if z + 1 < layers:
                total = total + 0.5 * (s_ref[sz, z + 1] - low)
            else:
                total = total - 0.5 * low
            value = v_ref[component, z] + COURANT * total
            o_ref[component, z] = value
            c_ref[:, k : k + 1] = value[:, 0:1]
            c_ref[:, half + k : half + k + 1] = value[:, width - 1 : width]


def stress_step(v_ref, prev_ref, next_ref, low_ref, high_ref, col_ref, w_ref, s_ref, y_ref, o_ref):
    layers = v_ref.shape[1]
    half = 3 * layers
    for z in range(layers):
        dx, dy, dz = [], [], []
        for c in range(3):
            before, after = strike_edges(low_ref, prev_ref, high_ref, next_ref, c, c, z)
            k = c * layers + z
            dx.append(rows_diff(v_ref[c, z], before, after))
            dy.append(
                cols_diff(v_ref[c, z], col_ref[:, k : k + 1], col_ref[:, half + k : half + k + 1])
            )
            low = w_ref[c] if z == 0 else v_ref[c, z - 1]
            if z + 1 < layers:
                dz.append(0.5 * (v_ref[c, z + 1] - low))
            else:
                dz.append(-0.5 * low)
        dilation = dx[0] + dy[1] + dz[2]
        xx = s_ref[0, z] + COURANT * (dilation + 2.0 * dx[0])
        yy = s_ref[1, z] + COURANT * (dilation + 2.0 * dy[1])
        zz = s_ref[2, z] + COURANT * (dilation + 2.0 * dz[2])
        xy = s_ref[3, z] + COURANT * (dy[0] + dx[1])
        xz = s_ref[4, z] + COURANT * (dz[0] + dx[2])
        yz = s_ref[5, z] + COURANT * (dz[1] + dy[2])
        pressure = (xx + yy + zz) / 3.0
        xx, yy, zz = xx - pressure, yy - pressure, zz - pressure
        shear = jnp.sqrt(0.5 * (xx * xx + yy * yy + zz * zz) + (xy * xy + xz * xz + yz * yz))
        limit = y_ref[z] + FRICTION * jnp.maximum(-pressure, 0.0)
        factor = limit / jnp.maximum(shear, limit)
        o_ref[0, z] = pressure + factor * xx
        o_ref[1, z] = pressure + factor * yy
        o_ref[2, z] = pressure + factor * zz
        o_ref[3, z] = factor * xy
        o_ref[4, z] = factor * xz
        o_ref[5, z] = factor * yz


def whole_block(shape):
    return pl.BlockSpec(shape, lambda *_: (0,) * len(shape))


def component_block(shape, dim):
    block = tuple(1 if d == dim else n for d, n in enumerate(shape))
    return pl.BlockSpec(block, lambda c: tuple(c if d == dim else 0 for d in range(len(shape))))


def struct(shape):
    return jax.ShapeDtypeStruct(shape, F32)


def cost(flops, *arrays):
    moved = sum(math.prod(a.shape) * a.dtype.itemsize for a in arrays)
    return pl.CostEstimate(flops=int(flops), bytes_accessed=int(moved), transcendentals=0)


def ring(axis):
    count = lax.axis_size(axis)
    forward = [(i, (i + 1) % count) for i in range(count)]
    return forward, [(b, a) for a, b in forward]


def exchange(block, axis):
    return lax.all_to_all(block, axis, split_axis=0, concat_axis=0)


def edges(first, last, axis):
    forward, backward = ring(axis)
    return lax.ppermute(last, axis, forward), lax.ppermute(first, axis, backward)


def fault_traction(interface, now, past, tables, scale):
    strike_count, dip_count = lax.axis_size("bx"), lax.axis_size("by")
    count, cells, width = interface.shape
    rows, modes = cells // strike_count, cells // dip_count
    strike_tw, strike_table, dip_tw, dip_table = tables
    block = interface.reshape(count, strike_count, rows, width).transpose(1, 0, 2, 3)
    block = exchange(block, "bx")
    wide = struct((strike_count, 2, count, rows, width))
    tall = struct((dip_count, 2, count, modes, width))
    block = pl.pallas_call(
        partial(strike_forward, strike_count),
        out_shape=wide,
        cost_estimate=cost(wide.size * 2 * strike_count, block, wide),
        name="strike_forward",
    )(block)
    block = exchange(block, "bx")

    def cells_dft(block, sign, out):
        return pl.pallas_call(
            partial(strike_cells_dft, sign),
            grid=(count,),
            in_specs=[
                component_block(block.shape, 2),
                whole_block(strike_tw.shape),
                whole_block(strike_table.shape),
            ],
            out_specs=component_block(out.shape, 2),
            out_shape=out,
            scratch_shapes=[pltpu.VMEM((2, cells, width), F32)],
            cost_estimate=cost(24 * count * cells * cells * width, block, out),
            name="strike_cells",
        )(block, strike_tw, strike_table)

    block = exchange(cells_dft(block, -1.0, tall), "by")
    block = pl.pallas_call(
        partial(dip_response, scale),
        grid=(count,),
        in_specs=[
            component_block(block.shape, 2),
            whole_block(dip_tw.shape),
            whole_block(dip_table.shape),
            whole_block(now.shape),
            component_block(past.shape, 1),
        ],
        out_specs=component_block(tall.shape, 2),
        out_shape=tall,
        scratch_shapes=[pltpu.VMEM((2, cells, width), F32)],
        cost_estimate=cost(48 * count * cells * width * width, block, tall, past, now),
        name="dip_response",
    )(block, dip_tw, dip_table, now, past)
    block = exchange(block, "by")
    block = exchange(cells_dft(block, 1.0, wide), "bx")
    flat = struct((strike_count, count, rows, width))
    block = pl.pallas_call(
        partial(strike_inverse, strike_count, scale),
        out_shape=flat,
        cost_estimate=cost(wide.size * 2 * strike_count, block, flat),
        name="strike_inverse",
    )(block)
    block = exchange(block, "bx")
    return block.transpose(1, 0, 2, 3).reshape(count, cells, width)


def tile_spec(shape, tile):
    block = shape[:-2] + (tile, shape[-1])
    lead = (0,) * (len(shape) - 2)
    return pl.BlockSpec(block, lambda i: lead + (i, 0))


def halo_specs(shape, tile):
    block = shape[:-2] + (8, shape[-1])
    lead = (0,) * (len(shape) - 2)
    step, last = tile // 8, shape[-2] // 8 - 1
    return [
        pl.BlockSpec(block, lambda i: lead + (jnp.maximum(i * step - 1, 0), 0)),
        pl.BlockSpec(block, lambda i: lead + (jnp.minimum((i + 1) * step, last), 0)),
    ]


def local(interface_velocity, history, kernel, velocity, stress, cohesion):
    strike_count, dip_count = lax.axis_size("bx"), lax.axis_size("by")
    _, layers, cells, width = velocity.shape
    strike_length, dip_length = cells * strike_count, width * dip_count
    scale = 1.0 / math.sqrt(strike_length * dip_length)
    angle = (2.0 * math.pi / strike_length) * (
        jnp.arange(cells, dtype=jnp.int32) * lax.axis_index("bx")
    ).astype(F32)
    strike_tw = jnp.stack([jnp.cos(angle), jnp.sin(angle)], axis=1)
    lane = np.outer(np.arange(dip_count), np.arange(width)) * (2.0 * math.pi / dip_length)
    dip_tw = jnp.asarray(np.stack([np.cos(lane), np.sin(lane)]).astype(np.float32))
    tables = (strike_tw, square_table(cells), dip_tw, square_table(width))

    past = kernel[1] * history[0]
    for h in range(1, history.shape[0]):
        past = past + kernel[h + 1] * history[h]
    modes = history.shape[3]
    past = past.reshape(2, 3, modes, dip_count, width).transpose(0, 1, 3, 2, 4)
    past = past.reshape(2, 3, cells, width)
    now = kernel[0].reshape(modes, dip_count, width).transpose(1, 0, 2).reshape(cells, width)

    step = 3 // CHUNKS
    traction = jnp.concatenate(
        [
            fault_traction(
                interface_velocity[c : c + step], now, past[:, c : c + step], tables, scale
            )
            for c in range(0, 3, step)
        ],
        axis=0,
    )

    tile = min(32, cells)
    grid = (cells // tile,)
    col_shape = (cells, 6 * layers)

    def columns(first, last):
        low, high = edges(first, last, "by")
        return jnp.concatenate([low, high], axis=1)

    def side(position):
        flat = [stress[c, :, :, position] for c in (3, 1, 5)]
        return jnp.concatenate(flat, axis=0).T

    def line(position):
        return jnp.stack([stress[c, :, position, :] for c in (0, 3, 4)])

    cols = columns(side(0), side(width - 1))
    low, high = edges(line(0), line(cells - 1), "bx")
    velocity_new, new_cols = pl.pallas_call(
        velocity_step,
        grid=grid,
        in_specs=[
            tile_spec(stress.shape, tile),
            *halo_specs(stress.shape, tile),
            whole_block(low.shape),
            whole_block(high.shape),
            tile_spec(col_shape, tile),
            tile_spec(velocity.shape, tile),
            tile_spec(traction.shape, tile),
        ],
        out_specs=[tile_spec(velocity.shape, tile), tile_spec(col_shape, tile)],
        out_shape=[struct(velocity.shape), struct(col_shape)],
        cost_estimate=cost(1e7, stress, velocity, velocity),
        name="velocity_step",
    )(stress, stress, stress, low, high, cols, velocity, traction)
    half = 3 * layers
    cols = columns(new_cols[:, :half], new_cols[:, half:])
    low, high = edges(velocity_new[:, :, 0], velocity_new[:, :, cells - 1], "bx")
    stress_new = pl.pallas_call(
        stress_step,
        grid=grid,
        in_specs=[
            tile_spec(velocity.shape, tile),
            *halo_specs(velocity.shape, tile),
            whole_block(low.shape),
            whole_block(high.shape),
            tile_spec(col_shape, tile),
            tile_spec(interface_velocity.shape, tile),
            tile_spec(stress.shape, tile),
            tile_spec(cohesion.shape, tile),
        ],
        out_specs=tile_spec(stress.shape, tile),
        out_shape=struct(stress.shape),
        cost_estimate=cost(2e7, stress, stress, velocity),
        name="stress_step",
    )(velocity_new, velocity_new, velocity_new, low, high, cols, interface_velocity, stress, cohesion)
    return velocity_new, stress_new


def solution(mesh):
    return jax.shard_map(
        local,
        mesh=mesh,
        in_specs=(
            P(None, "bx", "by"),
            P(None, None, None, "by", "bx", None, None),
            P(None, "by", "bx", None, None),
            P(None, None, "bx", "by"),
            P(None, None, "bx", "by"),
            P(None, "bx", "by"),
        ),
        out_specs=(P(None, None, "bx", "by"), P(None, None, "bx", "by")),
        check_vma=False,
    )
```

```python
from functools import partial
import math

import jax
import jax.numpy as jnp
import numpy as np
from jax import lax
from jax.experimental import pallas as pl
from jax.experimental.pallas import tpu as pltpu
from jax.sharding import PartitionSpec as P

COURANT = 0.3
FRICTION = 0.6
F32 = jnp.float32
BF16 = jnp.bfloat16


def halves(table):
    high = np.asarray(table, np.float32).astype(BF16)
    low = (np.asarray(table, np.float64) - high.astype(np.float64)).astype(BF16)
    return np.stack([high, low])


def square_table(length):
    index = np.arange(length)
    angle = 2.0 * math.pi / length * (index[:, None] * index[None, :] % length)
    return jnp.asarray(np.stack([halves(np.cos(angle)), halves(np.sin(angle))]))


def split(value):
    high = value.astype(BF16)
    return high, (value - high.astype(F32)).astype(BF16)


def product(value, table, left):
    def dot(a, b):
        if left:
            a, b = b, a
        return lax.dot_general(a, b, (((1,), (0,)), ((), ())), preferred_element_type=F32)

    return dot(value[0], table[0]) + (dot(value[0], table[1]) + dot(value[1], table[0]))


def complex_product(real_part, imag_part, table_ref, sign, left):
    cos = (table_ref[0, 0], table_ref[0, 1])
    sin = (table_ref[1, 0], table_ref[1, 1])
    real_part, imag_part = split(real_part), split(imag_part)
    return (
        product(real_part, cos, left) - sign * product(imag_part, sin, left),
        product(imag_part, cos, left) + sign * product(real_part, sin, left),
    )


def root(index, count):
    angle = 2.0 * math.pi * (index % count) / count
    cos, sin = math.cos(angle), math.sin(angle)
    return [float(round(v)) if abs(v - round(v)) < 1e-12 else v for v in (cos, sin)]


def add_term(total, factor, value):
    if factor == 0.0:
        return total
    term = value if factor == 1.0 else (-value if factor == -1.0 else factor * value)
    return term if total is None else total + term


def strike_forward(count, x_ref, o_ref):
    for r in range(count):
        real_part = imag_part = None
        for b in range(count):
            cos, sin = root(r * b, count)
            real_part = add_term(real_part, cos, x_ref[b])
            imag_part = add_term(imag_part, -sin, x_ref[b])
        o_ref[r, 0] = real_part
        o_ref[r, 1] = jnp.zeros_like(real_part) if imag_part is None else imag_part


def strike_inverse(count, scale, x_ref, o_ref):
    for b in range(count):
        total = None
        for r in range(count):
            cos, sin = root(r * b, count)
            total = add_term(total, cos, x_ref[r, 0])
            total = add_term(total, -sin, x_ref[r, 1])
        o_ref[b] = scale * total


def strike_cells_dft(sign, x_ref, tw_ref, table_ref, o_ref, held):
    blocks, _, rows, _ = x_ref.shape
    for s in range(blocks):
        for z in range(2):
            held[z, pl.ds(s * rows, rows), :] = x_ref[s, z]
    cos, sin = tw_ref[:, 0:1], sign * tw_ref[:, 1:2]
    real_part, imag_part = held[0], held[1]
    if sign < 0:
        real_part, imag_part = (
            real_part * cos - imag_part * sin,
            real_part * sin + imag_part * cos,
        )
    real_part, imag_part = complex_product(real_part, imag_part, table_ref, sign, True)
    if sign > 0:
        real_part, imag_part = (
            real_part * cos - imag_part * sin,
            real_part * sin + imag_part * cos,
        )
    held[0] = real_part
    held[1] = imag_part
    blocks, _, rows, _ = o_ref.shape
    for s in range(blocks):
        for z in range(2):
            o_ref[s, z] = held[z, pl.ds(s * rows, rows), :]


def dip_response(scale, x_ref, tw_ref, table_ref, now_ref, past_ref, o_ref, held):
    count, _, rows, _ = x_ref.shape
    for l in range(count):
        real_part = imag_part = None
        for j in range(count):
            cos, sin = root(l * j, count)
            real_part = add_term(real_part, cos, x_ref[j, 0])
            real_part = add_term(real_part, sin, x_ref[j, 1])
            imag_part = add_term(imag_part, cos, x_ref[j, 1])
            imag_part = add_term(imag_part, -sin, x_ref[j, 0])
        cos, sin = tw_ref[0, l : l + 1, :], tw_ref[1, l : l + 1, :]
        held[0, pl.ds(l * rows, rows), :] = real_part * cos + imag_part * sin
        held[1, pl.ds(l * rows, rows), :] = imag_part * cos - real_part * sin
    real_part, imag_part = complex_product(held[0], held[1], table_ref, -1.0, False)
    weight = scale * now_ref[...]
    real_part = weight * real_part + past_ref[0]
    imag_part = weight * imag_part + past_ref[1]
    real_part, imag_part = complex_product(real_part, imag_part, table_ref, 1.0, False)
    held[0] = real_part
    held[1] = imag_part
    for l in range(count):
        cos, sin = tw_ref[0, l : l + 1, :], tw_ref[1, l : l + 1, :]
        real_part = held[0, pl.ds(l * rows, rows), :]
        imag_part = held[1, pl.ds(l * rows, rows), :]
        held[0, pl.ds(l * rows, rows), :] = real_part * cos - imag_part * sin
        held[1, pl.ds(l * rows, rows), :] = imag_part * cos + real_part * sin
    for j in range(count):
        real_part = imag_part = None
        for l in range(count):
            cos, sin = root(l * j, count)
            lr = held[0, pl.ds(l * rows, rows), :]
            li = held[1, pl.ds(l * rows, rows), :]
            real_part = add_term(real_part, cos, lr)
            real_part = add_term(real_part, -sin, li)
            imag_part = add_term(imag_part, cos, li)
            imag_part = add_term(imag_part, sin, lr)
        o_ref[j, 0] = real_part
        o_ref[j, 1] = imag_part


def rows_diff(value, before, after):
    count = value.shape[0]
    row = lax.broadcasted_iota(jnp.int32, value.shape, 0)
    low = jnp.where(row == 0, before, pltpu.roll(value, 1, 0))
    high = jnp.where(row == count - 1, after, pltpu.roll(value, count - 1, 0))
    return 0.5 * (high - low)


def cols_diff(value, before, after):
    count = value.shape[1]
    col = lax.broadcasted_iota(jnp.int32, value.shape, 1)
    low = jnp.where(col == 0, before, pltpu.roll(value, 1, 1))
    high = jnp.where(col == count - 1, after, pltpu.roll(value, count - 1, 1))
    return 0.5 * (high - low)


def strike_edges(low_ref, prev_ref, high_ref, next_ref, slot, component, z):
    i, last = pl.program_id(0), pl.num_programs(0) - 1
    before = jnp.where(i == 0, low_ref[slot, z : z + 1, :], prev_ref[component, z, 7:8, :])
    after = jnp.where(i == last, high_ref[slot, z : z + 1, :], next_ref[component, z, 0:1, :])
    return before, after


def velocity_step(s_ref, prev_ref, next_ref, low_ref, high_ref, col_ref, v_ref, t_ref, o_ref, c_ref, l_ref, h_ref):
    layers = v_ref.shape[1]
    width = v_ref.shape[3]
    half = 3 * layers
    for component, (sx, sy, sz) in enumerate(((0, 3, 4), (3, 1, 5), (4, 5, 2))):
        for z in range(layers):
            before, after = strike_edges(low_ref, prev_ref, high_ref, next_ref, component, sx, z)
            total = rows_diff(s_ref[sx, z], before, after)
            k = component * layers + z
            total = total + cols_diff(
                s_ref[sy, z], col_ref[:, k : k + 1], col_ref[:, half + k : half + k + 1]
            )
            low = t_ref[component] if z == 0 else s_ref[sz, z - 1]
            if z + 1 < layers:
                total = total + 0.5 * (s_ref[sz, z + 1] - low)
            else:
                total = total - 0.5 * low
            value = v_ref[component, z] + COURANT * total
            o_ref[component, z] = value
            c_ref[:, k : k + 1] = value[:, 0:1]
            c_ref[:, half + k : half + k + 1] = value[:, width - 1 : width]

            @pl.when(pl.program_id(0) == 0)
            def _():
                l_ref[component, z : z + 1, :] = value[0:1, :]

            @pl.when(pl.program_id(0) == pl.num_programs(0) - 1)
            def _():
                h_ref[component, z : z + 1, :] = value[-1:, :]


def stress_step(v_ref, prev_ref, next_ref, low_ref, high_ref, col_ref, w_ref, s_ref, y_ref, o_ref):
    layers = v_ref.shape[1]
    half = 3 * layers
    for z in range(layers):
        dx, dy, dz = [], [], []
        for c in range(3):
            before, after = strike_edges(low_ref, prev_ref, high_ref, next_ref, c, c, z)
            k = c * layers + z
            dx.append(rows_diff(v_ref[c, z], before, after))
            dy.append(
                cols_diff(v_ref[c, z], col_ref[:, k : k + 1], col_ref[:, half + k : half + k + 1])
            )
            low = w_ref[c] if z == 0 else v_ref[c, z - 1]
            if z + 1 < layers:
                dz.append(0.5 * (v_ref[c, z + 1] - low))
            else:
                dz.append(-0.5 * low)
        dilation = dx[0] + dy[1] + dz[2]
        xx = s_ref[0, z] + COURANT * (dilation + 2.0 * dx[0])
        yy = s_ref[1, z] + COURANT * (dilation + 2.0 * dy[1])
        zz = s_ref[2, z] + COURANT * (dilation + 2.0 * dz[2])
        xy = s_ref[3, z] + COURANT * (dy[0] + dx[1])
        xz = s_ref[4, z] + COURANT * (dz[0] + dx[2])
        yz = s_ref[5, z] + COURANT * (dz[1] + dy[2])
        pressure = (xx + yy + zz) / 3.0
        xx, yy, zz = xx - pressure, yy - pressure, zz - pressure
        shear = jnp.sqrt(0.5 * (xx * xx + yy * yy + zz * zz) + (xy * xy + xz * xz + yz * yz))
        limit = y_ref[z] + FRICTION * jnp.maximum(-pressure, 0.0)
        factor = limit / jnp.maximum(shear, limit)
        o_ref[0, z] = pressure + factor * xx
        o_ref[1, z] = pressure + factor * yy
        o_ref[2, z] = pressure + factor * zz
        o_ref[3, z] = factor * xy
        o_ref[4, z] = factor * xz
        o_ref[5, z] = factor * yz


def whole_block(shape):
    return pl.BlockSpec(shape, lambda *_: (0,) * len(shape))


def struct(shape):
    return jax.ShapeDtypeStruct(shape, F32)


def cost(flops, *arrays):
    moved = sum(math.prod(a.shape) * a.dtype.itemsize for a in arrays)
    return pl.CostEstimate(flops=int(flops), bytes_accessed=int(moved), transcendentals=0)


def ring(axis):
    count = lax.axis_size(axis)
    forward = [(i, (i + 1) % count) for i in range(count)]
    return forward, [(b, a) for a, b in forward]


def edges(first, last, axis):
    forward, backward = ring(axis)
    return lax.ppermute(last, axis, forward), lax.ppermute(first, axis, backward)


def fault_kernel(
    scale,
    face_ref,
    strike_tw_ref,
    strike_table_ref,
    dip_tw_ref,
    dip_table_ref,
    now_ref,
    past_ref,
    o_ref,
    x1,
    b1,
    b2,
    t1,
    t2,
    u1,
    u2,
    w1,
    w2,
    y1,
    held,
    send_sem,
    recv_sem,
):
    count = face_ref.shape[0]
    sizes = {"bx": lax.axis_size("bx"), "by": lax.axis_size("by")}
    place = {"bx": lax.axis_index("bx"), "by": lax.axis_index("by")}

    def device(axis, target):
        if axis == "bx":
            return (target, place["by"])
        return (place["bx"], target)

    barrier = pltpu.get_barrier_semaphore()
    for axis in ("bx", "by"):

        @pl.loop(1, sizes[axis])
        def _(k):
            target = lax.rem(place[axis] + k, sizes[axis])
            pl.semaphore_signal(
                barrier, 1, device_id=device(axis, target), device_id_type=pl.DeviceIdType.MESH
            )

    pl.semaphore_wait(barrier, sizes["bx"] + sizes["by"] - 2)

    def copy(stage, axis, c, k, source, landing):
        me = place[axis]
        target = lax.rem(me + k, sizes[axis])
        return pltpu.make_async_remote_copy(
            src_ref=source.at[c, target],
            dst_ref=landing.at[c, me],
            send_sem=send_sem.at[stage, c, k],
            recv_sem=recv_sem.at[stage, c, k],
            device_id=device(axis, target),
            device_id_type=pl.DeviceIdType.MESH,
        )

    def own(stage, axis, c, source, landing):
        me = place[axis]
        return pltpu.make_async_copy(
            source.at[c, me], landing.at[c, me], recv_sem.at[stage, c, 0]
        )

    def send(stage, axis, c, source, landing):
        @pl.loop(1, sizes[axis])
        def _(k):
            copy(stage, axis, c, k, source, landing).start()

        own(stage, axis, c, source, landing).start()

    def receive(stage, axis, c, source, landing):
        own(stage, axis, c, source, landing).wait()

        @pl.loop(1, sizes[axis])
        def _(k):
            copy(stage, axis, c, k, source, landing).wait()

    stages = (
        ("bx", face_ref, x1),
        ("bx", b1, b2),
        ("by", t1, t2),
        ("by", u1, u2),
        ("bx", w1, w2),
        ("bx", y1, o_ref),
    )

    @pl.loop(0, count)
    def _(c):
        send(0, stages[0][0], c, *stages[0][1:])

    def work(stage, c):
        if stage == 0:
            strike_forward(sizes["bx"], x1.at[c], b1.at[c])
        elif stage == 1:
            strike_cells_dft(-1.0, b2.at[c], strike_tw_ref, strike_table_ref, t1.at[c], held)
        elif stage == 2:
            dip_response(
                scale, t2.at[c], dip_tw_ref, dip_table_ref, now_ref, past_ref.at[c], u1.at[c], held
            )
        elif stage == 3:
            strike_cells_dft(1.0, u2.at[c], strike_tw_ref, strike_table_ref, w1.at[c], held)
        else:
            strike_inverse(sizes["bx"], scale, w2.at[c], y1.at[c])

    for stage in range(5):

        @pl.loop(0, count)
        def _(c):
            receive(stage, stages[stage][0], c, *stages[stage][1:])
            work(stage, c)
            send(stage + 1, stages[stage + 1][0], c, *stages[stage + 1][1:])

    @pl.loop(0, count)
    def _(c):
        receive(5, stages[5][0], c, *stages[5][1:])


def fault_traction(interface, now, past, tables, scale):
    strike_count, dip_count = lax.axis_size("bx"), lax.axis_size("by")
    count, cells, width = interface.shape
    rows, modes = cells // strike_count, cells // dip_count
    flat = (count, strike_count, rows, width)
    wide = (count, strike_count, 2, rows, width)
    tall = (count, dip_count, 2, modes, width)
    peers = max(strike_count, dip_count)
    operands = (interface.reshape(flat), *tables, now, past)
    out = pl.pallas_call(
        partial(fault_kernel, scale),
        out_shape=struct(flat),
        in_specs=[pl.BlockSpec(memory_space=pltpu.VMEM)] * len(operands),
        out_specs=pl.BlockSpec(memory_space=pltpu.VMEM),
        scratch_shapes=[
            *[pltpu.VMEM(s, F32) for s in (flat, wide, wide, tall, tall, tall, tall, wide, wide)],
            pltpu.VMEM(flat, F32),
            pltpu.VMEM((2, cells, width), F32),
            pltpu.SemaphoreType.DMA((6, count, peers)),
            pltpu.SemaphoreType.DMA((6, count, peers)),
        ],
        compiler_params=pltpu.CompilerParams(
            collective_id=0, has_side_effects=True, vmem_limit_bytes=60 * 1024 * 1024
        ),
        name="fault_traction",
    )(*operands)
    return out.reshape(count, cells, width)


def tile_spec(shape, tile):
    block = shape[:-2] + (tile, shape[-1])
    lead = (0,) * (len(shape) - 2)
    return pl.BlockSpec(block, lambda i: lead + (i, 0))


def halo_specs(shape, tile):
    block = shape[:-2] + (8, shape[-1])
    lead = (0,) * (len(shape) - 2)
    step, last = tile // 8, shape[-2] // 8 - 1
    return [
        pl.BlockSpec(block, lambda i: lead + (jnp.maximum(i * step - 1, 0), 0)),
        pl.BlockSpec(block, lambda i: lead + (jnp.minimum((i + 1) * step, last), 0)),
    ]


def local(interface_velocity, history, kernel, velocity, stress, cohesion):
    strike_count, dip_count = lax.axis_size("bx"), lax.axis_size("by")
    _, layers, cells, width = velocity.shape
    strike_length, dip_length = cells * strike_count, width * dip_count
    scale = 1.0 / math.sqrt(strike_length * dip_length)
    angle = (2.0 * math.pi / strike_length) * (
        jnp.arange(cells, dtype=jnp.int32) * lax.axis_index("bx")
    ).astype(F32)
    strike_tw = jnp.stack([jnp.cos(angle), jnp.sin(angle)], axis=1)
    lane = np.outer(np.arange(dip_count), np.arange(width)) * (2.0 * math.pi / dip_length)
    dip_tw = jnp.asarray(np.stack([np.cos(lane), np.sin(lane)]).astype(np.float32))
    tables = (strike_tw, square_table(cells), dip_tw, square_table(width))

    past = kernel[1] * history[0]
    for h in range(1, history.shape[0]):
        past = past + kernel[h + 1] * history[h]
    modes = history.shape[3]
    past = past.reshape(2, 3, modes, dip_count, width).transpose(1, 0, 3, 2, 4)
    past = past.reshape(3, 2, cells, width)
    now = kernel[0].reshape(modes, dip_count, width).transpose(1, 0, 2).reshape(cells, width)

    traction = fault_traction(interface_velocity, now, past, tables, scale)

    tile = min(32, cells)
    grid = (cells // tile,)
    col_shape = (cells, 6 * layers)

    def columns(first, last):
        low, high = edges(first, last, "by")
        return jnp.concatenate([low, high], axis=1)

    def side(position):
        flat = [stress[c, :, :, position] for c in (3, 1, 5)]
        return jnp.concatenate(flat, axis=0).T

    def line(position):
        return jnp.stack([stress[c, :, position, :] for c in (0, 3, 4)])

    cols = columns(side(0), side(width - 1))
    low, high = edges(line(0), line(cells - 1), "bx")
    velocity_new, new_cols, first, last = pl.pallas_call(
        velocity_step,
        grid=grid,
        in_specs=[
            tile_spec(stress.shape, tile),
            *halo_specs(stress.shape, tile),
            whole_block(low.shape),
            whole_block(high.shape),
            tile_spec(col_shape, tile),
            tile_spec(velocity.shape, tile),
            tile_spec(traction.shape, tile),
        ],
        out_specs=[
            tile_spec(velocity.shape, tile),
            tile_spec(col_shape, tile),
            whole_block(low.shape),
            whole_block(low.shape),
        ],
        out_shape=[struct(velocity.shape), struct(col_shape), struct(low.shape), struct(low.shape)],
        cost_estimate=cost(1e7, stress, velocity, velocity),
        name="velocity_step",
    )(stress, stress, stress, low, high, cols, velocity, traction)
    half = 3 * layers
    cols = columns(new_cols[:, :half], new_cols[:, half:])
    low, high = edges(first, last, "bx")
    stress_new = pl.pallas_call(
        stress_step,
        grid=grid,
        in_specs=[
            tile_spec(velocity.shape, tile),
            *halo_specs(velocity.shape, tile),
            whole_block(low.shape),
            whole_block(high.shape),
            tile_spec(col_shape, tile),
            tile_spec(interface_velocity.shape, tile),
            tile_spec(stress.shape, tile),
            tile_spec(cohesion.shape, tile),
        ],
        out_specs=tile_spec(stress.shape, tile),
        out_shape=struct(stress.shape),
        cost_estimate=cost(2e7, stress, stress, velocity),
        name="stress_step",
    )(velocity_new, velocity_new, velocity_new, low, high, cols, interface_velocity, stress, cohesion)
    return velocity_new, stress_new


def solution(mesh):
    return jax.shard_map(
        local,
        mesh=mesh,
        in_specs=(
            P(None, "bx", "by"),
            P(None, None, None, "by", "bx", None, None),
            P(None, "by", "bx", None, None),
            P(None, None, "bx", "by"),
            P(None, None, "bx", "by"),
            P(None, "bx", "by"),
        ),
        out_specs=(P(None, None, "bx", "by"), P(None, None, "bx", "by")),
        check_vma=False,
    )
```

```python
from functools import partial
import math

import jax
import jax.numpy as jnp
import numpy as np
from jax import lax
from jax.experimental import pallas as pl
from jax.experimental.pallas import tpu as pltpu
from jax.sharding import PartitionSpec as P

COURANT = 0.3
FRICTION = 0.6
F32 = jnp.float32
BF16 = jnp.bfloat16


def halves(table):
    high = np.asarray(table, np.float32).astype(BF16)
    low = (np.asarray(table, np.float64) - high.astype(np.float64)).astype(BF16)
    return np.stack([high, low])


def square_table(length):
    index = np.arange(length)
    angle = 2.0 * math.pi / length * (index[:, None] * index[None, :] % length)
    return jnp.asarray(np.stack([halves(np.cos(angle)), halves(np.sin(angle))]))


def split(value):
    high = value.astype(BF16)
    return high, (value - high.astype(F32)).astype(BF16)


def product(value, table, left):
    def dot(a, b):
        if left:
            a, b = b, a
        return lax.dot_general(a, b, (((1,), (0,)), ((), ())), preferred_element_type=F32)

    return dot(value[0], table[0]) + (dot(value[0], table[1]) + dot(value[1], table[0]))


def complex_product(real_part, imag_part, table_ref, sign, left):
    cos = (table_ref[0, 0], table_ref[0, 1])
    sin = (table_ref[1, 0], table_ref[1, 1])
    real_part, imag_part = split(real_part), split(imag_part)
    return (
        product(real_part, cos, left) - sign * product(imag_part, sin, left),
        product(imag_part, cos, left) + sign * product(real_part, sin, left),
    )


def root(index, count):
    angle = 2.0 * math.pi * (index % count) / count
    cos, sin = math.cos(angle), math.sin(angle)
    return [float(round(v)) if abs(v - round(v)) < 1e-12 else v for v in (cos, sin)]


def add_term(total, factor, value):
    if factor == 0.0:
        return total
    term = value if factor == 1.0 else (-value if factor == -1.0 else factor * value)
    return term if total is None else total + term


def strike_forward(count, x_ref, o_ref):
    for r in range(count):
        real_part = imag_part = None
        for b in range(count):
            cos, sin = root(r * b, count)
            real_part = add_term(real_part, cos, x_ref[b])
            imag_part = add_term(imag_part, -sin, x_ref[b])
        o_ref[r, 0] = real_part
        o_ref[r, 1] = jnp.zeros_like(real_part) if imag_part is None else imag_part


def strike_inverse(count, scale, x_ref, o_ref):
    for b in range(count):
        total = None
        for r in range(count):
            cos, sin = root(r * b, count)
            total = add_term(total, cos, x_ref[r, 0])
            total = add_term(total, -sin, x_ref[r, 1])
        o_ref[b] = scale * total


def strike_cells_dft(sign, x_ref, tw_ref, table_ref, o_ref, held):
    blocks, _, rows, _ = x_ref.shape
    for s in range(blocks):
        for z in range(2):
            held[z, pl.ds(s * rows, rows), :] = x_ref[s, z]
    cos, sin = tw_ref[:, 0:1], sign * tw_ref[:, 1:2]
    real_part, imag_part = held[0], held[1]
    if sign < 0:
        real_part, imag_part = (
            real_part * cos - imag_part * sin,
            real_part * sin + imag_part * cos,
        )
    real_part, imag_part = complex_product(real_part, imag_part, table_ref, sign, True)
    if sign > 0:
        real_part, imag_part = (
            real_part * cos - imag_part * sin,
            real_part * sin + imag_part * cos,
        )
    held[0] = real_part
    held[1] = imag_part
    blocks, _, rows, _ = o_ref.shape
    for s in range(blocks):
        for z in range(2):
            o_ref[s, z] = held[z, pl.ds(s * rows, rows), :]


def dip_response(scale, x_refs, tw_ref, table_ref, now_ref, past_ref, o_refs, held):
    count, _, rows, width = x_refs[0].shape
    for h, x_ref in enumerate(x_refs):
        part = slice(h * width, (h + 1) * width)
        for l in range(count):
            real_part = imag_part = None
            for j in range(count):
                cos, sin = root(l * j, count)
                real_part = add_term(real_part, cos, x_ref[j, 0])
                real_part = add_term(real_part, sin, x_ref[j, 1])
                imag_part = add_term(imag_part, cos, x_ref[j, 1])
                imag_part = add_term(imag_part, -sin, x_ref[j, 0])
            cos, sin = tw_ref[0, l : l + 1, part], tw_ref[1, l : l + 1, part]
            held[0, pl.ds(l * rows, rows), part] = real_part * cos + imag_part * sin
            held[1, pl.ds(l * rows, rows), part] = imag_part * cos - real_part * sin
    real_part, imag_part = complex_product(held[0], held[1], table_ref, -1.0, False)
    weight = scale * now_ref[...]
    real_part = weight * real_part + past_ref[0]
    imag_part = weight * imag_part + past_ref[1]
    real_part, imag_part = complex_product(real_part, imag_part, table_ref, 1.0, False)
    held[0] = real_part
    held[1] = imag_part
    for l in range(count):
        cos, sin = tw_ref[0, l : l + 1, :], tw_ref[1, l : l + 1, :]
        real_part = held[0, pl.ds(l * rows, rows), :]
        imag_part = held[1, pl.ds(l * rows, rows), :]
        held[0, pl.ds(l * rows, rows), :] = real_part * cos - imag_part * sin
        held[1, pl.ds(l * rows, rows), :] = imag_part * cos + real_part * sin
    for h, o_ref in enumerate(o_refs):
        part = slice(h * width, (h + 1) * width)
        for j in range(count):
            real_part = imag_part = None
            for l in range(count):
                cos, sin = root(l * j, count)
                lr = held[0, pl.ds(l * rows, rows), part]
                li = held[1, pl.ds(l * rows, rows), part]
                real_part = add_term(real_part, cos, lr)
                real_part = add_term(real_part, -sin, li)
                imag_part = add_term(imag_part, cos, li)
                imag_part = add_term(imag_part, sin, lr)
            o_ref[j, 0] = real_part
            o_ref[j, 1] = imag_part


def rows_diff(value, before, after):
    count = value.shape[0]
    row = lax.broadcasted_iota(jnp.int32, value.shape, 0)
    low = jnp.where(row == 0, before, pltpu.roll(value, 1, 0))
    high = jnp.where(row == count - 1, after, pltpu.roll(value, count - 1, 0))
    return 0.5 * (high - low)


def cols_diff(value, before, after):
    count = value.shape[1]
    col = lax.broadcasted_iota(jnp.int32, value.shape, 1)
    low = jnp.where(col == 0, before, pltpu.roll(value, 1, 1))
    high = jnp.where(col == count - 1, after, pltpu.roll(value, count - 1, 1))
    return 0.5 * (high - low)


def strike_edges(low_ref, prev_ref, high_ref, next_ref, slot, component, z):
    i, last = pl.program_id(0), pl.num_programs(0) - 1
    before = jnp.where(i == 0, low_ref[slot, z : z + 1, :], prev_ref[component, z, 7:8, :])
    after = jnp.where(i == last, high_ref[slot, z : z + 1, :], next_ref[component, z, 0:1, :])
    return before, after


def velocity_step(s_ref, prev_ref, next_ref, low_ref, high_ref, col_ref, v_ref, t_ref, o_ref, c_ref, l_ref, h_ref):
    layers = v_ref.shape[1]
    width = v_ref.shape[3]
    half = 3 * layers
    for component, (sx, sy, sz) in enumerate(((0, 3, 4), (3, 1, 5), (4, 5, 2))):
        for z in range(layers):
            before, after = strike_edges(low_ref, prev_ref, high_ref, next_ref, component, sx, z)
            total = rows_diff(s_ref[sx, z], before, after)
            k = component * layers + z
            total = total + cols_diff(
                s_ref[sy, z], col_ref[:, k : k + 1], col_ref[:, half + k : half + k + 1]
            )
            low = t_ref[component] if z == 0 else s_ref[sz, z - 1]
            if z + 1 < layers:
                total = total + 0.5 * (s_ref[sz, z + 1] - low)
            else:
                total = total - 0.5 * low
            value = v_ref[component, z] + COURANT * total
            o_ref[component, z] = value
            c_ref[:, k : k + 1] = value[:, 0:1]
            c_ref[:, half + k : half + k + 1] = value[:, width - 1 : width]

            @pl.when(pl.program_id(0) == 0)
            def _():
                l_ref[component, z : z + 1, :] = value[0:1, :]

            @pl.when(pl.program_id(0) == pl.num_programs(0) - 1)
            def _():
                h_ref[component, z : z + 1, :] = value[-1:, :]


def stress_step(v_ref, prev_ref, next_ref, low_ref, high_ref, col_ref, w_ref, s_ref, y_ref, o_ref):
    layers = v_ref.shape[1]
    half = 3 * layers
    for z in range(layers):
        dx, dy, dz = [], [], []
        for c in range(3):
            before, after = strike_edges(low_ref, prev_ref, high_ref, next_ref, c, c, z)
            k = c * layers + z
            dx.append(rows_diff(v_ref[c, z], before, after))
            dy.append(
                cols_diff(v_ref[c, z], col_ref[:, k : k + 1], col_ref[:, half + k : half + k + 1])
            )
            low = w_ref[c] if z == 0 else v_ref[c, z - 1]
            if z + 1 < layers:
                dz.append(0.5 * (v_ref[c, z + 1] - low))
            else:
                dz.append(-0.5 * low)
        dilation = dx[0] + dy[1] + dz[2]
        xx = s_ref[0, z] + COURANT * (dilation + 2.0 * dx[0])
        yy = s_ref[1, z] + COURANT * (dilation + 2.0 * dy[1])
        zz = s_ref[2, z] + COURANT * (dilation + 2.0 * dz[2])
        xy = s_ref[3, z] + COURANT * (dy[0] + dx[1])
        xz = s_ref[4, z] + COURANT * (dz[0] + dx[2])
        yz = s_ref[5, z] + COURANT * (dz[1] + dy[2])
        pressure = (xx + yy + zz) / 3.0
        xx, yy, zz = xx - pressure, yy - pressure, zz - pressure
        shear = jnp.sqrt(0.5 * (xx * xx + yy * yy + zz * zz) + (xy * xy + xz * xz + yz * yz))
        limit = y_ref[z] + FRICTION * jnp.maximum(-pressure, 0.0)
        factor = limit / jnp.maximum(shear, limit)
        o_ref[0, z] = pressure + factor * xx
        o_ref[1, z] = pressure + factor * yy
        o_ref[2, z] = pressure + factor * zz
        o_ref[3, z] = factor * xy
        o_ref[4, z] = factor * xz
        o_ref[5, z] = factor * yz


def whole_block(shape):
    return pl.BlockSpec(shape, lambda *_: (0,) * len(shape))


def struct(shape):
    return jax.ShapeDtypeStruct(shape, F32)


def cost(flops, *arrays):
    moved = sum(math.prod(a.shape) * a.dtype.itemsize for a in arrays)
    return pl.CostEstimate(flops=int(flops), bytes_accessed=int(moved), transcendentals=0)


def ring(axis):
    count = lax.axis_size(axis)
    forward = [(i, (i + 1) % count) for i in range(count)]
    return forward, [(b, a) for a, b in forward]


def edges(first, last, axis):
    forward, backward = ring(axis)
    return lax.ppermute(last, axis, forward), lax.ppermute(first, axis, backward)


def fault_kernel(
    scale,
    face_ref,
    strike_tw_ref,
    strike_table_ref,
    dip_tw_ref,
    dip_table_ref,
    now_ref,
    past_ref,
    o_ref,
    x1,
    b1,
    b2,
    t1,
    t2,
    u1,
    u2,
    w1,
    w2,
    y1,
    held,
    held_part,
    send_sem,
    recv_sem,
):
    count = face_ref.shape[0]
    sizes = {"bx": lax.axis_size("bx"), "by": lax.axis_size("by")}
    place = {"bx": lax.axis_index("bx"), "by": lax.axis_index("by")}

    def device(axis, target):
        if axis == "bx":
            return (target, place["by"])
        return (place["bx"], target)

    barrier = pltpu.get_barrier_semaphore()
    for axis in ("bx", "by"):

        @pl.loop(1, sizes[axis])
        def _(k):
            target = lax.rem(place[axis] + k, sizes[axis])
            pl.semaphore_signal(
                barrier, 1, device_id=device(axis, target), device_id_type=pl.DeviceIdType.MESH
            )

    pl.semaphore_wait(barrier, sizes["bx"] + sizes["by"] - 2)

    def copy(stage, axis, c, k, source, landing):
        me = place[axis]
        target = lax.rem(me + k, sizes[axis])
        return pltpu.make_async_remote_copy(
            src_ref=source.at[c, target],
            dst_ref=landing.at[c, me],
            send_sem=send_sem.at[stage, c, k],
            recv_sem=recv_sem.at[stage, c, k],
            device_id=device(axis, target),
            device_id_type=pl.DeviceIdType.MESH,
        )

    def own(stage, axis, c, source, landing):
        me = place[axis]
        return pltpu.make_async_copy(
            source.at[c, me], landing.at[c, me], recv_sem.at[stage, c, 0]
        )

    def send(stage, axis, c, source, landing):
        @pl.loop(1, sizes[axis])
        def _(k):
            copy(stage, axis, c, k, source, landing).start()

        own(stage, axis, c, source, landing).start()

    def receive(stage, axis, c, source, landing):
        own(stage, axis, c, source, landing).wait()

        @pl.loop(1, sizes[axis])
        def _(k):
            copy(stage, axis, c, k, source, landing).wait()

    stages = (
        ("bx", face_ref, x1),
        ("bx", b1, b2),
        ("by", t1, t2),
        ("by", u1, u2),
        ("bx", w1, w2),
        ("bx", y1, o_ref),
    )

    parts = count // past_ref.shape[0]

    def go(stage, g):
        axis, source, landing = stages[stage]
        send(stage, axis, g, source, landing)

    def take(stage, g):
        axis, source, landing = stages[stage]
        receive(stage, axis, g, source, landing)

    def enter(g):
        take(0, g)
        strike_forward(sizes["bx"], x1.at[g], b1.at[g])
        go(1, g)

    def across(g):
        take(1, g)
        strike_cells_dft(-1.0, b2.at[g], strike_tw_ref, strike_table_ref, t1.at[g], held_part)
        go(2, g)

    def back(g):
        take(3, g)
        strike_cells_dft(1.0, u2.at[g], strike_tw_ref, strike_table_ref, w1.at[g], held_part)
        go(4, g)

    def leave(g):
        take(4, g)
        strike_inverse(sizes["bx"], scale, w2.at[g], y1.at[g])
        go(5, g)

    go(0, 0)
    go(0, 1)
    enter(0)

    @pl.loop(0, count - 1)
    def _(g):
        @pl.when(g + 2 < count)
        def _():
            go(0, g + 2)

        enter(g + 1)
        across(g)

    across(count - 1)

    @pl.loop(0, past_ref.shape[0])
    def _(c):
        for h in range(parts):
            take(2, c * parts + h)
        dip_response(
            scale,
            [t2.at[c * parts + h] for h in range(parts)],
            dip_tw_ref,
            dip_table_ref,
            now_ref,
            past_ref.at[c],
            [u1.at[c * parts + h] for h in range(parts)],
            held,
        )
        for h in range(parts):
            go(3, c * parts + h)

    back(0)

    @pl.loop(1, count)
    def _(g):
        back(g)
        leave(g - 1)

    leave(count - 1)

    @pl.loop(0, count)
    def _(g):
        take(5, g)


def fault_traction(interface, now, past, tables, scale):
    strike_count, dip_count = lax.axis_size("bx"), lax.axis_size("by")
    count, cells, width = interface.shape
    rows, modes = cells // strike_count, cells // dip_count
    parts = 2 if width % 256 == 0 else 1
    narrow = width // parts
    face = interface.reshape(count, strike_count, rows, parts, narrow).transpose(0, 3, 1, 2, 4)
    chunks = count * parts
    flat = (chunks, strike_count, rows, narrow)
    wide = (chunks, strike_count, 2, rows, narrow)
    tall = (chunks, dip_count, 2, modes, narrow)
    peers = max(strike_count, dip_count)
    operands = (face.reshape(flat), *tables, now, past)
    out = pl.pallas_call(
        partial(fault_kernel, scale),
        out_shape=struct(flat),
        in_specs=[pl.BlockSpec(memory_space=pltpu.VMEM)] * len(operands),
        out_specs=pl.BlockSpec(memory_space=pltpu.VMEM),
        scratch_shapes=[
            *[pltpu.VMEM(s, F32) for s in (flat, wide, wide, tall, tall, tall, tall, wide, wide)],
            pltpu.VMEM(flat, F32),
            pltpu.VMEM((2, cells, width), F32),
            pltpu.VMEM((2, cells, narrow), F32),
            pltpu.SemaphoreType.DMA((6, chunks, peers)),
            pltpu.SemaphoreType.DMA((6, chunks, peers)),
        ],
        compiler_params=pltpu.CompilerParams(
            collective_id=0, has_side_effects=True, vmem_limit_bytes=60 * 1024 * 1024
        ),
        name="fault_traction",
    )(*operands)
    out = out.reshape(count, parts, cells, narrow).transpose(0, 2, 1, 3)
    return out.reshape(count, cells, width)


def tile_spec(shape, tile):
    block = shape[:-2] + (tile, shape[-1])
    lead = (0,) * (len(shape) - 2)
    return pl.BlockSpec(block, lambda i: lead + (i, 0))


def halo_specs(shape, tile):
    block = shape[:-2] + (8, shape[-1])
    lead = (0,) * (len(shape) - 2)
    step, last = tile // 8, shape[-2] // 8 - 1
    return [
        pl.BlockSpec(block, lambda i: lead + (jnp.maximum(i * step - 1, 0), 0)),
        pl.BlockSpec(block, lambda i: lead + (jnp.minimum((i + 1) * step, last), 0)),
    ]


def local(interface_velocity, history, kernel, velocity, stress, cohesion):
    strike_count, dip_count = lax.axis_size("bx"), lax.axis_size("by")
    _, layers, cells, width = velocity.shape
    strike_length, dip_length = cells * strike_count, width * dip_count
    scale = 1.0 / math.sqrt(strike_length * dip_length)
    angle = (2.0 * math.pi / strike_length) * (
        jnp.arange(cells, dtype=jnp.int32) * lax.axis_index("bx")
    ).astype(F32)
    strike_tw = jnp.stack([jnp.cos(angle), jnp.sin(angle)], axis=1)
    lane = np.outer(np.arange(dip_count), np.arange(width)) * (2.0 * math.pi / dip_length)
    dip_tw = jnp.asarray(np.stack([np.cos(lane), np.sin(lane)]).astype(np.float32))
    tables = (strike_tw, square_table(cells), dip_tw, square_table(width))

    past = kernel[1] * history[0]
    for h in range(1, history.shape[0]):
        past = past + kernel[h + 1] * history[h]
    modes = history.shape[3]
    past = past.reshape(2, 3, modes, dip_count, width).transpose(1, 0, 3, 2, 4)
    past = past.reshape(3, 2, cells, width)
    now = kernel[0].reshape(modes, dip_count, width).transpose(1, 0, 2).reshape(cells, width)

    traction = fault_traction(interface_velocity, now, past, tables, scale)

    tile = min(32, cells)
    grid = (cells // tile,)
    col_shape = (cells, 6 * layers)

    def columns(first, last):
        low, high = edges(first, last, "by")
        return jnp.concatenate([low, high], axis=1)

    def side(position):
        flat = [stress[c, :, :, position] for c in (3, 1, 5)]
        return jnp.concatenate(flat, axis=0).T

    def line(position):
        return jnp.stack([stress[c, :, position, :] for c in (0, 3, 4)])

    cols = columns(side(0), side(width - 1))
    low, high = edges(line(0), line(cells - 1), "bx")
    velocity_new, new_cols, first, last = pl.pallas_call(
        velocity_step,
        grid=grid,
        in_specs=[
            tile_spec(stress.shape, tile),
            *halo_specs(stress.shape, tile),
            whole_block(low.shape),
            whole_block(high.shape),
            tile_spec(col_shape, tile),
            tile_spec(velocity.shape, tile),
            tile_spec(traction.shape, tile),
        ],
        out_specs=[
            tile_spec(velocity.shape, tile),
            tile_spec(col_shape, tile),
            whole_block(low.shape),
            whole_block(low.shape),
        ],
        out_shape=[struct(velocity.shape), struct(col_shape), struct(low.shape), struct(low.shape)],
        cost_estimate=cost(1e7, stress, velocity, velocity),
        name="velocity_step",
    )(stress, stress, stress, low, high, cols, velocity, traction)
    half = 3 * layers
    cols = columns(new_cols[:, :half], new_cols[:, half:])
    low, high = edges(first, last, "bx")
    stress_new = pl.pallas_call(
        stress_step,
        grid=grid,
        in_specs=[
            tile_spec(velocity.shape, tile),
            *halo_specs(velocity.shape, tile),
            whole_block(low.shape),
            whole_block(high.shape),
            tile_spec(col_shape, tile),
            tile_spec(interface_velocity.shape, tile),
            tile_spec(stress.shape, tile),
            tile_spec(cohesion.shape, tile),
        ],
        out_specs=tile_spec(stress.shape, tile),
        out_shape=struct(stress.shape),
        cost_estimate=cost(2e7, stress, stress, velocity),
        name="stress_step",
    )(velocity_new, velocity_new, velocity_new, low, high, cols, interface_velocity, stress, cohesion)
    return velocity_new, stress_new


def solution(mesh):
    return jax.shard_map(
        local,
        mesh=mesh,
        in_specs=(
            P(None, "bx", "by"),
            P(None, None, None, "by", "bx", None, None),
            P(None, "by", "bx", None, None),
            P(None, None, "bx", "by"),
            P(None, None, "bx", "by"),
            P(None, "bx", "by"),
        ),
        out_specs=(P(None, None, "bx", "by"), P(None, None, "bx", "by")),
        check_vma=False,
    )
```

```python
from functools import partial
import math

import jax
import jax.numpy as jnp
import numpy as np
from jax import lax
from jax.experimental import pallas as pl
from jax.experimental.pallas import tpu as pltpu
from jax.sharding import PartitionSpec as P

COURANT = 0.3
FRICTION = 0.6
F32 = jnp.float32
BF16 = jnp.bfloat16


def halves(table):
    high = np.asarray(table, np.float32).astype(BF16)
    low = (np.asarray(table, np.float64) - high.astype(np.float64)).astype(BF16)
    return np.stack([high, low])


def square_table(length):
    index = np.arange(length)
    angle = 2.0 * math.pi / length * (index[:, None] * index[None, :] % length)
    return jnp.asarray(np.stack([halves(np.cos(angle)), halves(np.sin(angle))]))


def split(value):
    high = value.astype(BF16)
    return high, (value - high.astype(F32)).astype(BF16)


def product(value, table, left):
    def dot(a, b):
        if left:
            a, b = b, a
        return lax.dot_general(a, b, (((1,), (0,)), ((), ())), preferred_element_type=F32)

    return dot(value[0], table[0]) + (dot(value[0], table[1]) + dot(value[1], table[0]))


def complex_product(real_part, imag_part, table_ref, sign, left):
    cos = (table_ref[0, 0], table_ref[0, 1])
    sin = (table_ref[1, 0], table_ref[1, 1])
    real_part, imag_part = split(real_part), split(imag_part)
    return (
        product(real_part, cos, left) - sign * product(imag_part, sin, left),
        product(imag_part, cos, left) + sign * product(real_part, sin, left),
    )


def root(index, count):
    angle = 2.0 * math.pi * (index % count) / count
    cos, sin = math.cos(angle), math.sin(angle)
    return [float(round(v)) if abs(v - round(v)) < 1e-12 else v for v in (cos, sin)]


def add_term(total, factor, value):
    if factor == 0.0:
        return total
    term = value if factor == 1.0 else (-value if factor == -1.0 else factor * value)
    return term if total is None else total + term


def strike_forward(count, x_ref, o_ref):
    for r in range(count):
        real_part = imag_part = None
        for b in range(count):
            cos, sin = root(r * b, count)
            real_part = add_term(real_part, cos, x_ref[b])
            imag_part = add_term(imag_part, -sin, x_ref[b])
        o_ref[r, 0] = real_part
        o_ref[r, 1] = jnp.zeros_like(real_part) if imag_part is None else imag_part


def strike_inverse(count, scale, x_ref, o_ref):
    for b in range(count):
        total = None
        for r in range(count):
            cos, sin = root(r * b, count)
            total = add_term(total, cos, x_ref[r, 0])
            total = add_term(total, -sin, x_ref[r, 1])
        o_ref[b] = scale * total


def strike_cells_dft(sign, x_ref, tw_ref, table_ref, o_ref, held):
    blocks, _, rows, _ = x_ref.shape
    for s in range(blocks):
        for z in range(2):
            held[z, pl.ds(s * rows, rows), :] = x_ref[s, z]
    cos, sin = tw_ref[:, 0:1], sign * tw_ref[:, 1:2]
    real_part, imag_part = held[0], held[1]
    if sign < 0:
        real_part, imag_part = (
            real_part * cos - imag_part * sin,
            real_part * sin + imag_part * cos,
        )
    real_part, imag_part = complex_product(real_part, imag_part, table_ref, sign, True)
    if sign > 0:
        real_part, imag_part = (
            real_part * cos - imag_part * sin,
            real_part * sin + imag_part * cos,
        )
    held[0] = real_part
    held[1] = imag_part
    blocks, _, rows, _ = o_ref.shape
    for s in range(blocks):
        for z in range(2):
            o_ref[s, z] = held[z, pl.ds(s * rows, rows), :]


def dip_response(scale, x_refs, tw_ref, table_ref, now_ref, past_ref, o_refs, held):
    count, _, rows, width = x_refs[0].shape
    for h, x_ref in enumerate(x_refs):
        part = slice(h * width, (h + 1) * width)
        for l in range(count):
            real_part = imag_part = None
            for j in range(count):
                cos, sin = root(l * j, count)
                real_part = add_term(real_part, cos, x_ref[j, 0])
                real_part = add_term(real_part, sin, x_ref[j, 1])
                imag_part = add_term(imag_part, cos, x_ref[j, 1])
                imag_part = add_term(imag_part, -sin, x_ref[j, 0])
            cos, sin = tw_ref[0, l : l + 1, part], tw_ref[1, l : l + 1, part]
            held[0, pl.ds(l * rows, rows), part] = real_part * cos + imag_part * sin
            held[1, pl.ds(l * rows, rows), part] = imag_part * cos - real_part * sin
    real_part, imag_part = complex_product(held[0], held[1], table_ref, -1.0, False)
    weight = scale * now_ref[...]
    real_part = weight * real_part + past_ref[0]
    imag_part = weight * imag_part + past_ref[1]
    real_part, imag_part = complex_product(real_part, imag_part, table_ref, 1.0, False)
    held[0] = real_part
    held[1] = imag_part
    for l in range(count):
        cos, sin = tw_ref[0, l : l + 1, :], tw_ref[1, l : l + 1, :]
        real_part = held[0, pl.ds(l * rows, rows), :]
        imag_part = held[1, pl.ds(l * rows, rows), :]
        held[0, pl.ds(l * rows, rows), :] = real_part * cos - imag_part * sin
        held[1, pl.ds(l * rows, rows), :] = imag_part * cos + real_part * sin
    for h, o_ref in enumerate(o_refs):
        part = slice(h * width, (h + 1) * width)
        for j in range(count):
            real_part = imag_part = None
            for l in range(count):
                cos, sin = root(l * j, count)
                lr = held[0, pl.ds(l * rows, rows), part]
                li = held[1, pl.ds(l * rows, rows), part]
                real_part = add_term(real_part, cos, lr)
                real_part = add_term(real_part, -sin, li)
                imag_part = add_term(imag_part, cos, li)
                imag_part = add_term(imag_part, sin, lr)
            o_ref[j, 0] = real_part
            o_ref[j, 1] = imag_part


def rows_diff(value, before, after):
    count = value.shape[0]
    row = lax.broadcasted_iota(jnp.int32, value.shape, 0)
    low = jnp.where(row == 0, before, pltpu.roll(value, 1, 0))
    high = jnp.where(row == count - 1, after, pltpu.roll(value, count - 1, 0))
    return 0.5 * (high - low)


def cols_diff(value, before, after):
    count = value.shape[1]
    col = lax.broadcasted_iota(jnp.int32, value.shape, 1)
    low = jnp.where(col == 0, before, pltpu.roll(value, 1, 1))
    high = jnp.where(col == count - 1, after, pltpu.roll(value, count - 1, 1))
    return 0.5 * (high - low)


def strike_edges(low_ref, prev_ref, high_ref, next_ref, slot, component, z):
    i, last = pl.program_id(0), pl.num_programs(0) - 1
    before = jnp.where(i == 0, low_ref[slot, z : z + 1, :], prev_ref[component, z, 7:8, :])
    after = jnp.where(i == last, high_ref[slot, z : z + 1, :], next_ref[component, z, 0:1, :])
    return before, after


def velocity_step(s_ref, prev_ref, next_ref, low_ref, high_ref, col_ref, v_ref, t_ref, o_ref, c_ref, l_ref, h_ref):
    layers = v_ref.shape[1]
    width = v_ref.shape[3]
    half = 3 * layers
    for component, (sx, sy, sz) in enumerate(((0, 3, 4), (3, 1, 5), (4, 5, 2))):
        for z in range(layers):
            before, after = strike_edges(low_ref, prev_ref, high_ref, next_ref, component, sx, z)
            total = rows_diff(s_ref[sx, z], before, after)
            k = component * layers + z
            total = total + cols_diff(
                s_ref[sy, z], col_ref[:, k : k + 1], col_ref[:, half + k : half + k + 1]
            )
            low = t_ref[component] if z == 0 else s_ref[sz, z - 1]
            if z + 1 < layers:
                total = total + 0.5 * (s_ref[sz, z + 1] - low)
            else:
                total = total - 0.5 * low
            value = v_ref[component, z] + COURANT * total
            o_ref[component, z] = value
            c_ref[:, k : k + 1] = value[:, 0:1]
            c_ref[:, half + k : half + k + 1] = value[:, width - 1 : width]

            @pl.when(pl.program_id(0) == 0)
            def _():
                l_ref[component, z : z + 1, :] = value[0:1, :]

            @pl.when(pl.program_id(0) == pl.num_programs(0) - 1)
            def _():
                h_ref[component, z : z + 1, :] = value[-1:, :]


def stress_step(v_ref, prev_ref, next_ref, low_ref, high_ref, col_ref, w_ref, s_ref, y_ref, o_ref):
    layers = v_ref.shape[1]
    half = 3 * layers
    for z in range(layers):
        dx, dy, dz = [], [], []
        for c in range(3):
            before, after = strike_edges(low_ref, prev_ref, high_ref, next_ref, c, c, z)
            k = c * layers + z
            dx.append(rows_diff(v_ref[c, z], before, after))
            dy.append(
                cols_diff(v_ref[c, z], col_ref[:, k : k + 1], col_ref[:, half + k : half + k + 1])
            )
            low = w_ref[c] if z == 0 else v_ref[c, z - 1]
            if z + 1 < layers:
                dz.append(0.5 * (v_ref[c, z + 1] - low))
            else:
                dz.append(-0.5 * low)
        dilation = dx[0] + dy[1] + dz[2]
        xx = s_ref[0, z] + COURANT * (dilation + 2.0 * dx[0])
        yy = s_ref[1, z] + COURANT * (dilation + 2.0 * dy[1])
        zz = s_ref[2, z] + COURANT * (dilation + 2.0 * dz[2])
        xy = s_ref[3, z] + COURANT * (dy[0] + dx[1])
        xz = s_ref[4, z] + COURANT * (dz[0] + dx[2])
        yz = s_ref[5, z] + COURANT * (dz[1] + dy[2])
        pressure = (xx + yy + zz) / 3.0
        xx, yy, zz = xx - pressure, yy - pressure, zz - pressure
        shear = jnp.sqrt(0.5 * (xx * xx + yy * yy + zz * zz) + (xy * xy + xz * xz + yz * yz))
        limit = y_ref[z] + FRICTION * jnp.maximum(-pressure, 0.0)
        factor = limit / jnp.maximum(shear, limit)
        o_ref[0, z] = pressure + factor * xx
        o_ref[1, z] = pressure + factor * yy
        o_ref[2, z] = pressure + factor * zz
        o_ref[3, z] = factor * xy
        o_ref[4, z] = factor * xz
        o_ref[5, z] = factor * yz


def whole_block(shape):
    return pl.BlockSpec(shape, lambda *_: (0,) * len(shape))


def struct(shape):
    return jax.ShapeDtypeStruct(shape, F32)


def cost(flops, *arrays):
    moved = sum(math.prod(a.shape) * a.dtype.itemsize for a in arrays)
    return pl.CostEstimate(flops=int(flops), bytes_accessed=int(moved), transcendentals=0)


def ring(axis):
    count = lax.axis_size(axis)
    forward = [(i, (i + 1) % count) for i in range(count)]
    return forward, [(b, a) for a, b in forward]


def edges(first, last, axis):
    forward, backward = ring(axis)
    return lax.ppermute(last, axis, forward), lax.ppermute(first, axis, backward)


def fault_kernel(
    scale,
    face_ref,
    strike_tw_ref,
    strike_table_ref,
    dip_tw_ref,
    dip_table_ref,
    now_ref,
    past_ref,
    o_ref,
    x1,
    b1,
    b2,
    t1,
    t2,
    u1,
    u2,
    w1,
    w2,
    y1,
    held,
    held_part,
    send_sem,
    recv_sem,
):
    count, narrow = x1.shape[0], x1.shape[-1]
    parts = count // past_ref.shape[0]
    sizes = {"bx": lax.axis_size("bx"), "by": lax.axis_size("by")}
    place = {"bx": lax.axis_index("bx"), "by": lax.axis_index("by")}

    def device(axis, target):
        if axis == "bx":
            return (target, place["by"])
        return (place["bx"], target)

    barrier = pltpu.get_barrier_semaphore()
    for axis in ("bx", "by"):

        @pl.loop(1, sizes[axis])
        def _(k):
            target = lax.rem(place[axis] + k, sizes[axis])
            pl.semaphore_signal(
                barrier, 1, device_id=device(axis, target), device_id_type=pl.DeviceIdType.MESH
            )

    pl.semaphore_wait(barrier, sizes["bx"] + sizes["by"] - 2)

    def piece(ref, g, slot):
        if len(ref.shape) == 4 and ref.shape[0] != count:
            return ref.at[g // parts, slot, :, pl.ds(pl.multiple_of(g % parts * narrow, narrow), narrow)]
        if ref is face_ref or ref is o_ref:
            return ref.at[g, slot, :, pl.ds(0, narrow)]
        return ref.at[g, slot]

    def copy(stage, axis, c, k, source, landing):
        me = place[axis]
        target = lax.rem(me + k, sizes[axis])
        return pltpu.make_async_remote_copy(
            src_ref=piece(source, c, target),
            dst_ref=piece(landing, c, me),
            send_sem=send_sem.at[stage, c, k],
            recv_sem=recv_sem.at[stage, c, k],
            device_id=device(axis, target),
            device_id_type=pl.DeviceIdType.MESH,
        )

    def own(stage, axis, c, source, landing):
        me = place[axis]
        return pltpu.make_async_copy(
            piece(source, c, me), piece(landing, c, me), recv_sem.at[stage, c, 0]
        )

    def send(stage, axis, c, source, landing):
        @pl.loop(1, sizes[axis])
        def _(k):
            copy(stage, axis, c, k, source, landing).start()

        own(stage, axis, c, source, landing).start()

    def receive(stage, axis, c, source, landing):
        own(stage, axis, c, source, landing).wait()

        @pl.loop(1, sizes[axis])
        def _(k):
            copy(stage, axis, c, k, source, landing).wait()

    stages = (
        ("bx", face_ref, x1),
        ("bx", b1, b2),
        ("by", t1, t2),
        ("by", u1, u2),
        ("bx", w1, w2),
        ("bx", y1, o_ref),
    )

    def go(stage, g):
        axis, source, landing = stages[stage]
        send(stage, axis, g, source, landing)

    def take(stage, g):
        axis, source, landing = stages[stage]
        receive(stage, axis, g, source, landing)

    def enter(g):
        take(0, g)
        strike_forward(sizes["bx"], x1.at[g], b1.at[g])
        go(1, g)

    def across(g):
        take(1, g)
        strike_cells_dft(-1.0, b2.at[g], strike_tw_ref, strike_table_ref, t1.at[g], held_part)
        go(2, g)

    def back(g):
        take(3, g)
        strike_cells_dft(1.0, u2.at[g], strike_tw_ref, strike_table_ref, w1.at[g], held_part)
        go(4, g)

    def leave(g):
        take(4, g)
        strike_inverse(sizes["bx"], scale, w2.at[g], y1.at[g])
        go(5, g)

    go(0, 0)
    go(0, 1)

    @pl.loop(0, count + 1)
    def _(g):
        @pl.when(g < count)
        def _():
            enter(g)

        @pl.when(g + 2 < count)
        def _():
            go(0, g + 2)

        @pl.when(g > 0)
        def _():
            across(g - 1)

    @pl.loop(0, past_ref.shape[0])
    def _(c):
        for h in range(parts):
            take(2, c * parts + h)
        dip_response(
            scale,
            [t2.at[c * parts + h] for h in range(parts)],
            dip_tw_ref,
            dip_table_ref,
            now_ref,
            past_ref.at[c],
            [u1.at[c * parts + h] for h in range(parts)],
            held,
        )
        for h in range(parts):
            go(3, c * parts + h)

    @pl.loop(0, count + 1)
    def _(g):
        @pl.when(g < count)
        def _():
            back(g)

        @pl.when(g > 0)
        def _():
            leave(g - 1)

    @pl.loop(0, count)
    def _(g):
        take(5, g)


def fault_traction(interface, now, past, tables, scale):
    strike_count, dip_count = lax.axis_size("bx"), lax.axis_size("by")
    count, cells, width = interface.shape
    rows, modes = cells // strike_count, cells // dip_count
    parts = 2 if width % 256 == 0 else 1
    narrow = width // parts
    face = interface.reshape(count, strike_count, rows, width)
    chunks = count * parts
    flat = (chunks, strike_count, rows, narrow)
    wide = (chunks, strike_count, 2, rows, narrow)
    tall = (chunks, dip_count, 2, modes, narrow)
    peers = max(strike_count, dip_count)
    operands = (face, *tables, now, past)
    out = pl.pallas_call(
        partial(fault_kernel, scale),
        out_shape=struct(face.shape),
        in_specs=[pl.BlockSpec(memory_space=pltpu.VMEM)] * len(operands),
        out_specs=pl.BlockSpec(memory_space=pltpu.VMEM),
        scratch_shapes=[
            *[pltpu.VMEM(s, F32) for s in (flat, wide, wide, tall, tall, tall, tall, wide, wide)],
            pltpu.VMEM(flat, F32),
            pltpu.VMEM((2, cells, width), F32),
            pltpu.VMEM((2, cells, narrow), F32),
            pltpu.SemaphoreType.DMA((6, chunks, peers)),
            pltpu.SemaphoreType.DMA((6, chunks, peers)),
        ],
        compiler_params=pltpu.CompilerParams(
            collective_id=0, has_side_effects=True, vmem_limit_bytes=60 * 1024 * 1024
        ),
        name="fault_traction",
    )(*operands)
    return out.reshape(count, cells, width)


def tile_spec(shape, tile):
    block = shape[:-2] + (tile, shape[-1])
    lead = (0,) * (len(shape) - 2)
    return pl.BlockSpec(block, lambda i: lead + (i, 0))


def halo_specs(shape, tile):
    block = shape[:-2] + (8, shape[-1])
    lead = (0,) * (len(shape) - 2)
    step, last = tile // 8, shape[-2] // 8 - 1
    return [
        pl.BlockSpec(block, lambda i: lead + (jnp.maximum(i * step - 1, 0), 0)),
        pl.BlockSpec(block, lambda i: lead + (jnp.minimum((i + 1) * step, last), 0)),
    ]


def local(interface_velocity, history, kernel, velocity, stress, cohesion):
    strike_count, dip_count = lax.axis_size("bx"), lax.axis_size("by")
    _, layers, cells, width = velocity.shape
    strike_length, dip_length = cells * strike_count, width * dip_count
    scale = 1.0 / math.sqrt(strike_length * dip_length)
    angle = (2.0 * math.pi / strike_length) * (
        jnp.arange(cells, dtype=jnp.int32) * lax.axis_index("bx")
    ).astype(F32)
    strike_tw = jnp.stack([jnp.cos(angle), jnp.sin(angle)], axis=1)
    lane = np.outer(np.arange(dip_count), np.arange(width)) * (2.0 * math.pi / dip_length)
    dip_tw = jnp.asarray(np.stack([np.cos(lane), np.sin(lane)]).astype(np.float32))
    dip_table = lax.optimization_barrier(square_table(width))
    if width % cells == 0:
        strike_table = dip_table[:, :, :: width // cells, :cells]
    else:
        strike_table = square_table(cells)
    tables = (strike_tw, strike_table, dip_tw, dip_table)

    past = kernel[1] * history[0]
    for h in range(1, history.shape[0]):
        past = past + kernel[h + 1] * history[h]
    modes = history.shape[3]
    past = past.reshape(2, 3, modes, dip_count, width).transpose(1, 0, 3, 2, 4)
    past = past.reshape(3, 2, cells, width)
    now = kernel[0].reshape(modes, dip_count, width).transpose(1, 0, 2).reshape(cells, width)

    traction = fault_traction(interface_velocity, now, past, tables, scale)

    tile = min(32, cells)
    grid = (cells // tile,)
    col_shape = (cells, 6 * layers)

    def columns(first, last):
        low, high = edges(first, last, "by")
        return jnp.concatenate([low, high], axis=1)

    def side(position):
        flat = [stress[c, :, :, position] for c in (3, 1, 5)]
        return jnp.concatenate(flat, axis=0).T

    def line(position):
        return jnp.stack([stress[c, :, position, :] for c in (0, 3, 4)])

    cols = columns(side(0), side(width - 1))
    low, high = edges(line(0), line(cells - 1), "bx")
    velocity_new, new_cols, first, last = pl.pallas_call(
        velocity_step,
        grid=grid,
        in_specs=[
            tile_spec(stress.shape, tile),
            *halo_specs(stress.shape, tile),
            whole_block(low.shape),
            whole_block(high.shape),
            tile_spec(col_shape, tile),
            tile_spec(velocity.shape, tile),
            tile_spec(traction.shape, tile),
        ],
        out_specs=[
            tile_spec(velocity.shape, tile),
            tile_spec(col_shape, tile),
            whole_block(low.shape),
            whole_block(low.shape),
        ],
        out_shape=[struct(velocity.shape), struct(col_shape), struct(low.shape), struct(low.shape)],
        cost_estimate=cost(1e7, stress, velocity, velocity),
        name="velocity_step",
    )(stress, stress, stress, low, high, cols, velocity, traction)
    half = 3 * layers
    cols = columns(new_cols[:, :half], new_cols[:, half:])
    low, high = edges(first, last, "bx")
    stress_new = pl.pallas_call(
        stress_step,
        grid=grid,
        in_specs=[
            tile_spec(velocity.shape, tile),
            *halo_specs(velocity.shape, tile),
            whole_block(low.shape),
            whole_block(high.shape),
            tile_spec(col_shape, tile),
            tile_spec(interface_velocity.shape, tile),
            tile_spec(stress.shape, tile),
            tile_spec(cohesion.shape, tile),
        ],
        out_specs=tile_spec(stress.shape, tile),
        out_shape=struct(stress.shape),
        cost_estimate=cost(2e7, stress, stress, velocity),
        name="stress_step",
    )(velocity_new, velocity_new, velocity_new, low, high, cols, interface_velocity, stress, cohesion)
    return velocity_new, stress_new


def solution(mesh):
    return jax.shard_map(
        local,
        mesh=mesh,
        in_specs=(
            P(None, "bx", "by"),
            P(None, None, None, "by", "bx", None, None),
            P(None, "by", "bx", None, None),
            P(None, None, "bx", "by"),
            P(None, None, "bx", "by"),
            P(None, "bx", "by"),
        ),
        out_specs=(P(None, None, "bx", "by"), P(None, None, "bx", "by")),
        check_vma=False,
    )
```
